32 devices in a mesh: seq: 8 (over y, x, core), tp: 4 (over z).
Axes of the slice: x: 2, y: 2, z: 4, core: 2. Of those that a mesh axis runs over, the one named last changes fastest.
Arguments:
- conv_values: bfloat16 [2048, 8192], P('seq', 'tp'), may hold values from -6 to 6
- gate_values: bfloat16 [2048, 8192], P('seq', 'tp'), may hold values from -6 to 6
- conv_maps: bfloat16 [2048, 2048], P('seq'), may hold values from -6 to 6
- step_raw: float32 [2048, 128], P('seq', 'tp'), may hold values from -8 to 13
- decay_log: float32 [128], P('tp'), may hold values from -20 to 2
- skip_gain: float32 [128], P('tp'), may hold values from 0.5 to 1.5
- values_kernel: float32 [4, 8192], P(None, 'tp'), may hold values from -3 to 3
- values_offset: float32 [8192], P('tp'), may hold values from -0.5 to 0.5
- maps_kernel: float32 [4, 2048], replicated, may hold values from -3 to 3
- maps_offset: float32 [2048], replicated, may hold values from -0.5 to 0.5
- norm_weight: float32 [8192], P('tp'), may hold values from 0.5 to 1.5
- out_weight: bfloat16 [8192, 8192], P('tp', 'seq'), may hold values from -0.0625 to 0.0625
- residual: bfloat16 [2048, 8192], P(('seq', 'tp')), may hold values from -6 to 6
Outputs:
- mixed: float32 [2048, 8192], P(('seq', 'tp'))
The draws below stay inside these ranges and needn't reach their ends.
All inputs are finite; a program needn't handle non-finite values.
Results may differ from the reference program's by a relative error of at most 0.012.
Values may be sent and summed in bfloat16 or wider, within the bound.
A program may use at most 128 MiB of HBM per device.

```python
import jax
import jax.numpy as jnp
from jax import lax

D = 8192
HEADS = 128
HEAD_DIM = 64
STATE = 128
GROUPS = 8
CONV = 4
LARGE_STEP_COUNT = 3
L_DEV = 256
DI = 8192
TOKEN_COUNT = 2048
N_TP = 4


def head_rates(key):
    random_subkeys = jax.random.split(jax.random.fold_in(key, 11), 2)
    fast_share = 0.5
    chooser = jax.random.uniform(random_subkeys[0], (HEADS,), jnp.float32)
    spread = jax.random.uniform(random_subkeys[1], (HEADS,), jnp.float32, -0.35, 0.35)
    small_step_floor = 0.35 / (TOKEN_COUNT * 0.0078)
    head_rate = jnp.where(chooser < fast_share, 3.2, small_step_floor) * jnp.exp(spread)
    return (head_rate, small_step_floor)


def draw_decay_log(key, part):
    head_rate, small_step_floor = head_rates(key)
    return jnp.log(head_rate).astype(jnp.float32)


def draw_step_raw(key, part):
    head_rate, small_step_floor = head_rates(key)
    random_subkeys = jax.random.split(jax.random.fold_in(key, 23), 2)
    expected_output = jnp.exp(jax.random.uniform(random_subkeys[0], (TOKEN_COUNT, HEADS), jnp.float32, jnp.log(0.002), jnp.log(0.02)))
    large_step_rows = jax.random.randint(random_subkeys[1], (LARGE_STEP_COUNT,), 0, TOKEN_COUNT)
    token_positions = jnp.arange(TOKEN_COUNT, dtype=jnp.int32)
    inside_large_step = jnp.any(token_positions[:, None] == large_step_rows[None, :], axis=1)
    large_step_value = 0.25 / small_step_floor
    expected_output = jnp.where(inside_large_step[:, None], large_step_value, expected_output)
    return (expected_output + jnp.log(-jnp.expm1(-expected_output))).astype(jnp.float32)


def block_levels(stream_key, extent, cuts, smallest, largest):
    def one(dim, shards_of):
        draws = jax.random.uniform(jax.random.fold_in(jax.random.fold_in(stream_key, 6), dim), (shards_of,), jnp.float32, smallest / len(cuts), largest / len(cuts))
        return jnp.repeat(jnp.exp(draws), extent[dim] // shards_of).reshape((-1,) + (1,) * (len(extent) - dim - 1))

    loudness = one(*cuts[0])
    for cut in cuts[1:]:
        loudness = loudness * one(*cut)
    return loudness


def scatter_about(key, extent, deviation, bound, cuts=(), kind=jnp.bfloat16):
    array = jax.random.normal(key, extent, jnp.float32) * deviation
    if len(cuts) > 0:
        array = block_levels(key, extent, cuts, -0.22, 0.18) * array
    return jnp.clip(array, min=-bound, max=bound).astype(kind)


def setup_inputs(seed: int = 0) -> dict:
    keys = jax.random.split(jax.random.key(seed), 14)
    return {
        "conv_values": scatter_about(keys[0], (TOKEN_COUNT, DI), 1.0, 6.0, ((0, 8), (1, 4))),
        "gate_values": scatter_about(keys[1], (TOKEN_COUNT, DI), 1.0, 6.0, ((0, 8), (1, 4))),
        "conv_maps": scatter_about(keys[2], (TOKEN_COUNT, 2 * GROUPS * STATE), 1.0, 6.0, ((0, 8),)),
        "step_raw": draw_step_raw(jax.random.fold_in(keys[13], 71), 0),
        "decay_log": draw_decay_log(jax.random.fold_in(keys[13], 71), 0),
        "skip_gain": jnp.clip(0.5 + 1.0 * jax.random.uniform(keys[5], (HEADS,), jnp.float32) ** block_levels(keys[5], (HEADS,), ((0, 4),), -0.2, 0.2), 0.5, 1.5),
        "values_kernel": scatter_about(keys[6], (CONV, DI), CONV ** -0.5, 3.0, ((1, 4),), jnp.float32),
        "values_offset": jnp.clip(jax.random.uniform(keys[7], (DI,), jnp.float32, -0.5, 0.5) * block_levels(keys[7], (DI,), ((0, 4),), -0.4, 0.0), -0.5, 0.5),
        "maps_kernel": scatter_about(keys[8], (CONV, 2 * GROUPS * STATE), CONV ** -0.5, 3.0, (), jnp.float32),
        "maps_offset": jnp.clip(jax.random.uniform(keys[9], (2 * GROUPS * STATE,), jnp.float32, -0.5, 0.5), -0.5, 0.5),
        "norm_weight": jnp.clip(0.5 + 1.0 * jax.random.uniform(keys[10], (DI,), jnp.float32) ** block_levels(keys[10], (DI,), ((0, 4),), -0.2, 0.2), 0.5, 1.5),
        "out_weight": scatter_about(keys[11], (DI, D), DI ** -0.5, 0.0625, ((0, 4), (1, 8))),
        "residual": scatter_about(keys[12], (TOKEN_COUNT, D), 1.0, 6.0, ((0, 32),)),
    }


def causal_conv(signal, weight, offset):
    length = signal.shape[0]
    padded = jnp.concatenate([jnp.zeros((CONV - 1, signal.shape[1]), jnp.float32), signal.astype(jnp.float32)], axis=0)
    summed = offset[None, :] + weight[0][None, :] * padded[0:length]
    for position in range(1, CONV):
        summed = summed + weight[position][None, :] * padded[position:position + length]
    return jax.nn.silu(summed).astype(jnp.bfloat16)

def reference(conv_values, gate_values, conv_maps, step_raw, decay_log, skip_gain, values_kernel, values_offset, maps_kernel, maps_offset, norm_weight, out_weight, residual):
    highest = lax.Precision.HIGHEST
    values_conv = causal_conv(conv_values, values_kernel, values_offset)
    maps_conv = causal_conv(conv_maps, maps_kernel, maps_offset)
    step_size = jax.nn.softplus(step_raw)
    log_decay = -jnp.exp(decay_log)[None, :] * step_size
    per_group = HEADS // GROUPS
    block_count = TOKEN_COUNT // L_DEV
    value_blocks = values_conv.astype(jnp.float32).reshape(block_count, L_DEV, HEADS, HEAD_DIM)
    input_blocks = maps_conv[:, :GROUPS * STATE].astype(jnp.float32).reshape(block_count, L_DEV, GROUPS, STATE)
    output_blocks = maps_conv[:, GROUPS * STATE:].astype(jnp.float32).reshape(block_count, L_DEV, GROUPS, STATE)
    gate_blocks = gate_values.reshape(block_count, L_DEV, DI)
    step_blocks = step_size.reshape(block_count, L_DEV, HEADS)
    decay_blocks = log_decay.reshape(block_count, L_DEV, HEADS)
    residual_blocks = residual.reshape(block_count, L_DEV, D)
    weight_split = out_weight.astype(jnp.float32).reshape(N_TP, DI // N_TP, D)
    causal = jnp.tril(jnp.ones((L_DEV, L_DEV), dtype=bool))

    def block_step(carry_state, block_items):
        block_values, block_inputs, block_outputs, block_gate, block_step_size, block_decay, block_residual = block_items
        cum_log = jnp.cumsum(block_decay, axis=0)
        input_heads = jnp.repeat(block_inputs, per_group, axis=1)
        output_heads = jnp.repeat(block_outputs, per_group, axis=1)
        group_scores = jnp.einsum('tgn,sgn->gts', block_outputs, block_inputs, precision=highest)
        scores = jnp.repeat(group_scores, per_group, axis=0)
        gap_log = cum_log.T[:, :, None] - cum_log.T[:, None, :]
        kernel = jnp.where(causal[None], jnp.exp(jnp.where(causal[None], gap_log, 0.0)), 0.0)
        mixing = kernel * scores * block_step_size.T[:, None, :]
        within = jnp.einsum('hts,shp->thp', mixing, block_values, precision=highest)
        carried = jnp.einsum('thn,hpn->thp', output_heads, carry_state, precision=highest) * jnp.exp(cum_log)[:, :, None]
        mixer_out = within + carried + skip_gain[None, :, None] * block_values
        end_weight = jnp.exp(cum_log[-1][None, :] - cum_log) * block_step_size
        new_state = jnp.exp(cum_log[-1])[:, None, None] * carry_state + jnp.einsum('shp,shn->hpn', block_values * end_weight[:, :, None], input_heads, precision=highest)
        gated_out = mixer_out * jax.nn.silu(block_gate.astype(jnp.float32)).reshape(L_DEV, HEADS, HEAD_DIM)
        grouped = gated_out.reshape(L_DEV, GROUPS, per_group * HEAD_DIM)
        inv_rms = lax.rsqrt(lax.optimization_barrier(jnp.mean(grouped * grouped, axis=2, keepdims=True)) + 1e-05)
        normed = ((grouped * inv_rms).reshape(L_DEV, DI) * norm_weight[None, :]).astype(jnp.bfloat16)
        parts = jnp.einsum('qkc,kcd->qkd', normed.astype(jnp.float32).reshape(L_DEV, N_TP, DI // N_TP), weight_split)
        rounded = lax.optimization_barrier(parts.astype(jnp.bfloat16))
        mixed_block = block_residual.astype(jnp.float32) + lax.optimization_barrier(jnp.sum(rounded.astype(jnp.float32), axis=1))
        return (new_state, mixed_block)
    start_state = jnp.zeros((HEADS, HEAD_DIM, STATE), jnp.float32)
    final_state, mixed_blocks = lax.scan(block_step, start_state, (value_blocks, input_blocks, output_blocks, gate_blocks, step_blocks, decay_blocks, residual_blocks))
    return mixed_blocks.reshape(TOKEN_COUNT, D)
```

```python
import functools

import jax
import jax.numpy as jnp
from jax import lax
from jax.experimental import pallas as pl
from jax.experimental.pallas import tpu as pltpu
from jax.sharding import PartitionSpec as P

HEADS = 128
HEAD_DIM = 64
STATE = 128
GROUPS = 8
CONV = 4


def passed_along(array, axis, by):
    size = lax.axis_size(axis)
    pairs = [(i, i + by) for i in range(size) if 0 <= i + by < size]
    return lax.ppermute(array, axis, pairs)


def entering_2(value, axis, join, neutral):
    count, mine = (lax.axis_size(axis), lax.axis_index(axis))
    pieces = jax.tree.map(lambda part: lax.all_gather(part, axis), value)
    subtotal = jax.tree.map(
        lambda part, zero: jnp.full_like(part, 0) + jnp.asarray(zero, part.dtype), value, neutral
    )

    def turn(position, subtotal):
        longer = join(subtotal, jax.tree.map(lambda part: part[position], pieces))
        return jax.tree.map(lambda new, old: jnp.where(position < mine, new, old), longer, subtotal)

    return lax.fori_loop(0, count - 1, turn, subtotal)


def rim_conv(rim_rows, local_rows, kernel, offset):
    length = local_rows.shape[0]
    padded = jnp.concatenate([rim_rows.astype(jnp.float32), local_rows.astype(jnp.float32)], axis=0)
    summed = offset[None, :] + kernel[0][None, :] * padded[0:length]
    for position in range(1, CONV):
        summed = summed + kernel[position][None, :] * padded[position : position + length]
    return jax.nn.silu(summed).astype(jnp.bfloat16)


def ring_place(spot, size):
    if size % 4:
        return spot
    half = size // 2
    past = spot - half
    turned = half + (half - 2 - 2 * lax.div(past, 2)) + lax.rem(past, 2)
    return jnp.where(spot < half, spot, turned)


def mix_kernel(
    n, m, x_ref, w_ref, out_ref, gat, part, up, down,
    own_sem, gat_send, gat_recv, up_send, up_recv, down_send, down_recv, out_send, out_recv,
):
    mesh_ids = pl.DeviceIdType.MESH
    me, z = lax.axis_index("seq"), lax.axis_index("tp")
    spot = ring_place(me, n)
    right = ring_place(lax.rem(spot + 1, n), n)
    left = ring_place(lax.rem(spot + n - 1, n), n)
    half = gat.shape[2]
    depth = gat.shape[3]
    width = w_ref.shape[1]
    rows = part.shape[1] // m
    tile = min(width, 256)

    own = [
        pltpu.make_async_copy(x_ref.at[pl.ds(d * half, half)], gat.at[0, d], own_sem.at[d])
        for d in range(2)
    ]
    for copy in own:
        copy.start()

    barrier = pltpu.get_barrier_semaphore()

    def greet(step, carry):
        pl.semaphore_signal(
            barrier, inc=1, device_id=(lax.rem(me + step, n), z), device_id_type=mesh_ids
        )
        return carry

    lax.fori_loop(1, n, greet, 0)

    @pl.when(z > 0)
    def _():
        pl.semaphore_signal(barrier, inc=1, device_id=(me, z - 1), device_id_type=mesh_ids)

    @pl.when(z < m - 1)
    def _():
        pl.semaphore_signal(barrier, inc=1, device_id=(me, z + 1), device_id_type=mesh_ids)

    beside = (z > 0).astype(jnp.int32) + (z < m - 1).astype(jnp.int32)
    pl.semaphore_wait(barrier, n - 1 + beside)

    for copy in own:
        copy.wait()

    def gather_copy(step, d):
        return pltpu.make_async_remote_copy(
            src_ref=gat.at[step, d],
            dst_ref=gat.at[step + 1, d],
            send_sem=gat_send.at[step, d],
            recv_sem=gat_recv.at[step + 1, d],
            device_id=(right if d == 0 else left, z),
            device_id_type=mesh_ids,
        )

    def gather_arrival(step, d):
        return pltpu.make_async_remote_copy(
            src_ref=gat.at[step, d],
            dst_ref=gat.at[step, d],
            send_sem=gat_send.at[step, d],
            recv_sem=gat_recv.at[step, d],
            device_id=(right if d == 0 else left, z),
            device_id_type=mesh_ids,
        )

    def chain_copy(step, j, buffer, send, recv, to):
        return pltpu.make_async_remote_copy(
            src_ref=part.at[step, pl.ds(j * rows, rows)],
            dst_ref=buffer.at[step, pl.ds(j * rows, rows)],
            send_sem=send.at[step, j],
            recv_sem=recv.at[step, j],
            device_id=(me, to),
            device_id_type=mesh_ids,
        )

    def owner(step):
        there = jnp.where(z < m // 2, spot - step + n, spot + step)
        return ring_place(lax.rem(there, n), n)

    def out_copy(step, sender):
        return pltpu.make_async_remote_copy(
            src_ref=part.at[step, pl.ds(pl.multiple_of(z * rows, rows), rows)],
            dst_ref=out_ref.at[sender],
            send_sem=out_send.at[step],
            recv_sem=out_recv.at[sender],
            device_id=(owner(step), z),
            device_id_type=mesh_ids,
        )

    def added(step, j, buffer):
        span = pl.ds(j * rows, rows)
        part[step, span] = (
            part[step, span].astype(jnp.float32) + buffer[step, span].astype(jnp.float32)
        ).astype(jnp.bfloat16)

    up_lag, down_lag = z, m - 1 - z
    last_lag = jnp.maximum(up_lag, down_lag)

    def turn(tau, carry):
        @pl.when(tau < n)
        def _():
            @pl.when(tau > 0)
            def _():
                for d in range(2):
                    gather_arrival(tau, d).wait_recv()

            @pl.when(tau < n - 1)
            def _():
                for d in range(2):
                    gather_copy(tau, d).start()

            block = gat[tau].reshape(2 * half, depth)
            for c in range(0, width, tile):
                part[tau, :, c : c + tile] = jnp.dot(
                    block, w_ref[:, c : c + tile], preferred_element_type=jnp.float32
                ).astype(jnp.bfloat16)

        t_up = tau - up_lag

        @pl.when((t_up >= 0) & (t_up < n))
        def _():
            for j in range(m - 1, 0, -1):
                @pl.when(z < j)
                def _():
                    copy = chain_copy(t_up, j, up, up_send, up_recv, z + 1)

                    @pl.when(z > 0)
                    def _():
                        copy.wait_recv()
                        added(t_up, j, up)

                    copy.start()

        t_down = tau - down_lag

        @pl.when((t_down >= 0) & (t_down < n))
        def _():
            for j in range(m - 1):
                @pl.when(z > j)
                def _():
                    copy = chain_copy(t_down, j, down, down_send, down_recv, z - 1)

                    @pl.when(z < m - 1)
                    def _():
                        copy.wait_recv()
                        added(t_down, j, down)

                    copy.start()

        t_last = tau - last_lag

        @pl.when((t_last >= 0) & (t_last < n))
        def _():
            for j in range(m):
                @pl.when(z == j)
                def _():
                    span = pl.ds(j * rows, rows)
                    total = part[t_last, span].astype(jnp.float32)
                    if j > 0:
                        chain_copy(t_last, j, up, up_send, up_recv, z).wait_recv()
                        total = total + up[t_last, span].astype(jnp.float32)
                    if j < m - 1:
                        chain_copy(t_last, j, down, down_send, down_recv, z).wait_recv()
                        total = total + down[t_last, span].astype(jnp.float32)
                    part[t_last, span] = total.astype(jnp.bfloat16)

            @pl.when(t_last == 0)
            def _():
                out_ref[me] = part[0, pl.ds(pl.multiple_of(z * rows, rows), rows)]

            @pl.when(t_last > 0)
            def _():
                out_copy(t_last, me).start()

        return carry

    lax.fori_loop(0, n + m - 1, turn, 0)

    def finish(step, carry):
        @pl.when(step < n - 1)
        def _():
            for d in range(2):
                gather_copy(step, d).wait_send()

        for j in range(m):
            @pl.when(z < j)
            def _():
                chain_copy(step, j, up, up_send, up_recv, z).wait_send()

            @pl.when(z > j)
            def _():
                chain_copy(step, j, down, down_send, down_recv, z).wait_send()

        @pl.when(step > 0)
        def _():
            out_copy(step, me).wait_send()
            out_copy(step, lax.rem(me + step, n)).wait_recv()

        return carry

    lax.fori_loop(0, n, finish, 0)


def mix(normed, weight):
    n, m = lax.axis_size("seq"), lax.axis_size("tp")
    length, depth = normed.shape
    width = weight.shape[1]
    rows = length // m
    half = length // 2
    slots = pltpu.VMEM((n, length, width), jnp.bfloat16)
    dma = pltpu.SemaphoreType.DMA
    vmem = pl.BlockSpec(memory_space=pltpu.VMEM)
    return pl.pallas_call(
        functools.partial(mix_kernel, n, m),
        out_shape=jax.ShapeDtypeStruct((n, rows, width), jnp.bfloat16),
        in_specs=[pl.BlockSpec(memory_space=pl.ANY), vmem],
        out_specs=vmem,
        scratch_shapes=[
            pltpu.VMEM((n, 2, half, depth), jnp.bfloat16),
            slots,
            slots,
            slots,
            dma((2,)),
            dma((n, 2)),
            dma((n, 2)),
            dma((n, m)),
            dma((n, m)),
            dma((n, m)),
            dma((n, m)),
            dma((n,)),
            dma((n,)),
        ],
        compiler_params=pltpu.CompilerParams(
            collective_id=0, has_side_effects=True, vmem_limit_bytes=48 << 20
        ),
        cost_estimate=pl.CostEstimate(
            flops=2 * n * length * depth * width,
            bytes_accessed=2 * (depth * width + length * depth),
            transcendentals=0,
        ),
    )(normed, weight)


def shards(
    conv_values,
    gate_values,
    conv_maps,
    step_raw,
    decay_log,
    skip_gain,
    values_kernel,
    values_offset,
    maps_kernel,
    maps_offset,
    norm_weight,
    out_weight,
    residual,
):
    highest = lax.Precision.HIGHEST
    length = conv_values.shape[0]
    heads_dev = decay_log.shape[0]
    rim_count = CONV - 1
    rim_inner, rim_maps = passed_along(
        (conv_values[length - rim_count :], conv_maps[length - rim_count :]), "seq", 1
    )
    values_conv = rim_conv(rim_inner, conv_values, values_kernel, values_offset)
    maps_conv = rim_conv(rim_maps, conv_maps, maps_kernel, maps_offset)
    step_size = jax.nn.softplus(step_raw)
    log_decay = -jnp.exp(decay_log)[None, :] * step_size
    cum_log = jnp.cumsum(log_decay, axis=0)
    heads_here = lax.axis_index("tp") * heads_dev + jnp.arange(heads_dev, dtype=jnp.int32)
    group_of = heads_here * GROUPS // HEADS
    one_hot = (group_of[:, None] == jnp.arange(GROUPS, dtype=jnp.int32)[None, :]).astype(
        jnp.float32
    )
    input_groups = maps_conv[:, : GROUPS * STATE].astype(jnp.float32).reshape(length, GROUPS, STATE)
    output_groups = (
        maps_conv[:, GROUPS * STATE :].astype(jnp.float32).reshape(length, GROUPS, STATE)
    )
    input_heads = jnp.einsum("hg,qgn->qhn", one_hot, input_groups, precision=highest)
    output_heads = jnp.einsum("hg,qgn->qhn", one_hot, output_groups, precision=highest)
    value_heads = values_conv.astype(jnp.float32).reshape(length, heads_dev, HEAD_DIM)
    causal = jnp.tril(jnp.ones((length, length), dtype=bool))
    gap_log = cum_log.T[:, :, None] - cum_log.T[:, None, :]
    kernel = jnp.where(causal[None], jnp.exp(jnp.where(causal[None], gap_log, 0.0)), 0.0)
    scores = jnp.einsum("thn,shn->hts", output_heads, input_heads, precision=highest)
    mixing = kernel * scores * step_size.T[:, None, :]
    within = jnp.einsum("hts,shp->thp", mixing, value_heads, precision=highest)
    end_weight = jnp.exp(cum_log[-1][None, :] - cum_log) * step_size
    local_state = jnp.einsum(
        "shp,shn->hpn", value_heads * end_weight[:, :, None], input_heads, precision=highest
    )
    shard_decay = jnp.exp(cum_log[-1])
    zeros_state = jnp.zeros_like(local_state)

    def combine(earlier, latter):
        return (earlier[0] * latter[0], latter[0][:, None, None] * earlier[1] + latter[1])

    prefix = entering_2(
        (shard_decay, local_state), "seq", combine, (jnp.ones_like(shard_decay), zeros_state)
    )
    entering = prefix[1]
    carried = (
        jnp.einsum("thn,hpn->thp", output_heads, entering, precision=highest)
        * jnp.exp(cum_log)[:, :, None]
    )
    mixer_out = within + carried + skip_gain[None, :, None] * value_heads
    gated_out = mixer_out * jax.nn.silu(gate_values.astype(jnp.float32)).reshape(
        length, heads_dev, HEAD_DIM
    )
    head_squares = jnp.sum(gated_out * gated_out, axis=2)
    all_heads = lax.all_gather(head_squares, "tp", axis=1, tiled=True)
    group_totals = jnp.sum(all_heads.reshape(length, GROUPS, HEADS // GROUPS), axis=2)
    group_squares = jnp.einsum("qg,hg->qh", group_totals, one_hot, precision=highest)
    inv_rms = lax.rsqrt(group_squares / (HEADS // GROUPS * HEAD_DIM) + 1e-05)
    normed = (
        (gated_out * inv_rms[:, :, None]).reshape(length, heads_dev * HEAD_DIM)
        * norm_weight[None, :]
    ).astype(jnp.bfloat16)
    blocks = mix(normed, out_weight)
    summed = jnp.transpose(blocks, (1, 0, 2)).reshape(residual.shape).astype(jnp.float32)
    return residual.astype(jnp.float32) + summed


def solution(mesh):
    placed = (
        P("seq", "tp"),
        P("seq", "tp"),
        P("seq", None),
        P("seq", "tp"),
        P("tp"),
        P("tp"),
        P(None, "tp"),
        P("tp"),
        P(),
        P(),
        P("tp"),
        P("tp", "seq"),
        P(("seq", "tp"), None),
    )
    return jax.shard_map(
        shards, mesh=mesh, in_specs=placed, out_specs=P(("seq", "tp"), None), check_vma=False
    )
```

```python
import functools

import jax
import jax.numpy as jnp
from jax import lax
from jax.experimental import pallas as pl
from jax.experimental.pallas import tpu as pltpu
from jax.sharding import PartitionSpec as P

HEADS = 128
HEAD_DIM = 64
STATE = 128
GROUPS = 8
CONV = 4


def ring_place(spot, size):
    if size % 4:
        return spot
    half = size // 2
    past = spot - half
    turned = half + (half - 2 - 2 * lax.div(past, 2)) + lax.rem(past, 2)
    return jnp.where(spot < half, spot, turned)


def mix_kernel(
    n, m, x_ref, w_ref, out_ref, gat, part, up, down,
    own_sem, gat_send, gat_recv, up_send, up_recv, down_send, down_recv, out_send, out_recv,
):
    mesh_ids = pl.DeviceIdType.MESH
    me, z = lax.axis_index("seq"), lax.axis_index("tp")
    spot = ring_place(me, n)
    right = ring_place(lax.rem(spot + 1, n), n)
    left = ring_place(lax.rem(spot + n - 1, n), n)
    half = gat.shape[2]
    depth = gat.shape[3]
    width = w_ref.shape[1]
    rows = part.shape[1] // m
    tile = min(width, 256)

    own = [
        pltpu.make_async_copy(x_ref.at[pl.ds(d * half, half)], gat.at[0, d], own_sem.at[d])
        for d in range(2)
    ]
    for copy in own:
        copy.start()

    barrier = pltpu.get_barrier_semaphore()

    def greet(step, carry):
        pl.semaphore_signal(
            barrier, inc=1, device_id=(lax.rem(me + step, n), z), device_id_type=mesh_ids
        )
        return carry

    lax.fori_loop(1, n, greet, 0)

    @pl.when(z > 0)
    def _():
        pl.semaphore_signal(barrier, inc=1, device_id=(me, z - 1), device_id_type=mesh_ids)

    @pl.when(z < m - 1)
    def _():
        pl.semaphore_signal(barrier, inc=1, device_id=(me, z + 1), device_id_type=mesh_ids)

    beside = (z > 0).astype(jnp.int32) + (z < m - 1).astype(jnp.int32)
    pl.semaphore_wait(barrier, n - 1 + beside)

    for copy in own:
        copy.wait()

    def gather_copy(step, d):
        return pltpu.make_async_remote_copy(
            src_ref=gat.at[step, d],
            dst_ref=gat.at[step + 1, d],
            send_sem=gat_send.at[step, d],
            recv_sem=gat_recv.at[step + 1, d],
            device_id=(right if d == 0 else left, z),
            device_id_type=mesh_ids,
        )

    def gather_arrival(step, d):
        return pltpu.make_async_remote_copy(
            src_ref=gat.at[step, d],
            dst_ref=gat.at[step, d],
            send_sem=gat_send.at[step, d],
            recv_sem=gat_recv.at[step, d],
            device_id=(right if d == 0 else left, z),
            device_id_type=mesh_ids,
        )

    def chain_copy(step, j, buffer, send, recv, to):
        return pltpu.make_async_remote_copy(
            src_ref=part.at[step, pl.ds(j * rows, rows)],
            dst_ref=buffer.at[step, pl.ds(j * rows, rows)],
            send_sem=send.at[step, j],
            recv_sem=recv.at[step, j],
            device_id=(me, to),
            device_id_type=mesh_ids,
        )

    def owner(step):
        there = jnp.where(z < m // 2, spot - step + n, spot + step)
        return ring_place(lax.rem(there, n), n)

    def out_copy(step, sender):
        return pltpu.make_async_remote_copy(
            src_ref=part.at[step, pl.ds(pl.multiple_of(z * rows, rows), rows)],
            dst_ref=out_ref.at[sender],
            send_sem=out_send.at[step],
            recv_sem=out_recv.at[sender],
            device_id=(owner(step), z),
            device_id_type=mesh_ids,
        )

    def added(step, j, buffer):
        span = pl.ds(j * rows, rows)
        part[step, span] = (
            part[step, span].astype(jnp.float32) + buffer[step, span].astype(jnp.float32)
        ).astype(jnp.bfloat16)

    up_lag, down_lag = z, m - 1 - z
    last_lag = jnp.maximum(up_lag, down_lag)

    def turn(tau, carry):
        @pl.when(tau < n)
        def _():
            @pl.when(tau > 0)
            def _():
                for d in range(2):
                    gather_arrival(tau, d).wait_recv()

            @pl.when(tau < n - 1)
            def _():
                for d in range(2):
                    gather_copy(tau, d).start()

            block = gat[tau].reshape(2 * half, depth)
            for c in range(0, width, tile):
                part[tau, :, c : c + tile] = jnp.dot(
                    block, w_ref[:, c : c + tile], preferred_element_type=jnp.float32
                ).astype(jnp.bfloat16)

        t_up = tau - up_lag

        @pl.when((t_up >= 0) & (t_up < n))
        def _():
            for j in range(m - 1, 0, -1):
                @pl.when(z < j)
                def _():
                    copy = chain_copy(t_up, j, up, up_send, up_recv, z + 1)

                    @pl.when(z > 0)
                    def _():
                        copy.wait_recv()
                        added(t_up, j, up)

                    copy.start()

        t_down = tau - down_lag

        @pl.when((t_down >= 0) & (t_down < n))
        def _():
            for j in range(m - 1):
                @pl.when(z > j)
                def _():
                    copy = chain_copy(t_down, j, down, down_send, down_recv, z - 1)

                    @pl.when(z < m - 1)
                    def _():
                        copy.wait_recv()
                        added(t_down, j, down)

                    copy.start()

        t_last = tau - last_lag

        @pl.when((t_last >= 0) & (t_last < n))
        def _():
            for j in range(m):
                @pl.when(z == j)
                def _():
                    span = pl.ds(j * rows, rows)
                    total = part[t_last, span].astype(jnp.float32)
                    if j > 0:
                        chain_copy(t_last, j, up, up_send, up_recv, z).wait_recv()
                        total = total + up[t_last, span].astype(jnp.float32)
                    if j < m - 1:
                        chain_copy(t_last, j, down, down_send, down_recv, z).wait_recv()
                        total = total + down[t_last, span].astype(jnp.float32)
                    part[t_last, span] = total.astype(jnp.bfloat16)

            @pl.when(t_last == 0)
            def _():
                out_ref[me] = part[0, pl.ds(pl.multiple_of(z * rows, rows), rows)]

            @pl.when(t_last > 0)
            def _():
                out_copy(t_last, me).start()

        return carry

    lax.fori_loop(0, n + m - 1, turn, 0)

    def finish(step, carry):
        @pl.when(step < n - 1)
        def _():
            for d in range(2):
                gather_copy(step, d).wait_send()

        for j in range(m):
            @pl.when(z < j)
            def _():
                chain_copy(step, j, up, up_send, up_recv, z).wait_send()

            @pl.when(z > j)
            def _():
                chain_copy(step, j, down, down_send, down_recv, z).wait_send()

        @pl.when(step > 0)
        def _():
            out_copy(step, me).wait_send()
            out_copy(step, lax.rem(me + step, n)).wait_recv()

        return carry

    lax.fori_loop(0, n, finish, 0)


def mix(normed, weight):
    n, m = lax.axis_size("seq"), lax.axis_size("tp")
    length, depth = normed.shape
    width = weight.shape[1]
    rows = length // m
    half = length // 2
    slots = pltpu.VMEM((n, length, width), jnp.bfloat16)
    dma = pltpu.SemaphoreType.DMA
    vmem = pl.BlockSpec(memory_space=pltpu.VMEM)
    return pl.pallas_call(
        functools.partial(mix_kernel, n, m),
        out_shape=jax.ShapeDtypeStruct((n, rows, width), jnp.bfloat16),
        in_specs=[pl.BlockSpec(memory_space=pl.ANY), vmem],
        out_specs=vmem,
        scratch_shapes=[
            pltpu.VMEM((n, 2, half, depth), jnp.bfloat16),
            slots,
            slots,
            slots,
            dma((2,)),
            dma((n, 2)),
            dma((n, 2)),
            dma((n, m)),
            dma((n, m)),
            dma((n, m)),
            dma((n, m)),
            dma((n,)),
            dma((n,)),
        ],
        compiler_params=pltpu.CompilerParams(
            collective_id=0, has_side_effects=True, vmem_limit_bytes=48 << 20
        ),
        cost_estimate=pl.CostEstimate(
            flops=2 * n * length * depth * width,
            bytes_accessed=2 * (depth * width + length * depth),
            transcendentals=0,
        ),
    )(normed, weight)


def front_kernel(
    n, per_group, whole_groups, x_ref, gate_ref, maps_ref, cum_ref, cum_t_ref, step_ref, step_t_ref,
    decay_ref, skip_ref, taps_ref, base_ref, map_taps_ref, map_base_ref, gain_ref, out_ref,
    rim_x, rim_maps, pad, values, y, b_maps, c_maps, scores, local, arrived, leaving,
    rim_send, rim_recv, chain_send, chain_recv,
):
    mesh_ids = pl.DeviceIdType.MESH
    exact = lax.Precision.HIGHEST
    me, z = lax.axis_index("seq"), lax.axis_index("tp")
    length, channels = x_ref.shape
    heads = cum_ref.shape[1]
    groups_here = scores.shape[0]
    first_group = lax.div(z * heads, per_group)
    tile = arrived.shape[2]
    tiles = channels // tile
    group_width = channels // groups_here
    rim = rim_x.shape[0]

    barrier = pltpu.get_barrier_semaphore()
    has_left, has_right = me > 0, me < n - 1

    @pl.when(has_left)
    def _():
        pl.semaphore_signal(barrier, inc=1, device_id=(me - 1, z), device_id_type=mesh_ids)

    @pl.when(has_right)
    def _():
        pl.semaphore_signal(barrier, inc=1, device_id=(me + 1, z), device_id_type=mesh_ids)

    pl.semaphore_wait(barrier, has_left.astype(jnp.int32) + has_right.astype(jnp.int32))

    def rim_copy(which):
        source, target = ((x_ref, rim_x), (maps_ref, rim_maps))[which]
        return pltpu.make_async_remote_copy(
            src_ref=source.at[pl.ds(length - rim, rim)],
            dst_ref=target,
            send_sem=rim_send.at[which],
            recv_sem=rim_recv.at[which],
            device_id=(me + 1, z),
            device_id_type=mesh_ids,
        )

    @pl.when(has_right)
    def _():
        for which in range(2):
            rim_copy(which).start()

    @pl.when(has_left)
    def _():
        for which in range(2):
            rim_copy(which).wait_recv()

    @pl.when(jnp.logical_not(has_left))
    def _():
        rim_x[...] = jnp.zeros_like(rim_x)
        rim_maps[...] = jnp.zeros_like(rim_maps)

    def conv(rows_ref, rim_ref, taps, base, start, size):
        span = pl.ds(start, size)
        pad[0:rim, 0:size] = rim_ref[:, span].astype(jnp.float32)
        pad[rim : rim + length, 0:size] = rows_ref[:, span].astype(jnp.float32)
        total = base[:, span]
        for k in range(CONV):
            at = rim - (CONV - 1) + k
            total = total + taps[k : k + 1, span] * pad[at : at + length, 0:size]
        return jax.nn.silu(total).astype(jnp.bfloat16)

    for g in range(groups_here):
        at = pl.multiple_of((first_group + g) * STATE, STATE)
        b_maps[g] = conv(maps_ref, rim_maps, map_taps_ref, map_base_ref, at, STATE)
        at = pl.multiple_of((GROUPS + first_group + g) * STATE, STATE)
        c_maps[g] = conv(maps_ref, rim_maps, map_taps_ref, map_base_ref, at, STATE)
        scores[g] = lax.dot_general(
            c_maps[g], b_maps[g], (((1,), (1,)), ((), ())), preferred_element_type=jnp.float32
        )

    def spread(per_head, start):
        head = lax.broadcasted_iota(jnp.int32, (heads, tile), 0) * HEAD_DIM
        lane = lax.broadcasted_iota(jnp.int32, (heads, tile), 1) + start
        chosen = ((lane >= head) & (lane < head + HEAD_DIM)).astype(jnp.float32)
        return jnp.dot(
            per_head, chosen, precision=exact, preferred_element_type=jnp.float32
        )

    cum = cum_ref[...]
    end_weight = jnp.exp(cum[length - 1 : length] - cum) * step_ref[...]
    grown = jnp.exp(cum)

    def states(c, carry):
        start = pl.multiple_of(c * tile, tile)
        span = pl.ds(start, tile)
        value = conv(x_ref, rim_x, taps_ref, base_ref, start, tile)
        values[:, span] = value
        weighted = (value.astype(jnp.float32) * spread(end_weight, start)).astype(jnp.bfloat16)
        g = lax.div(start, group_width)
        local[c] = lax.dot_general(
            b_maps[g], weighted, (((0,), (0,)), ((), ())), preferred_element_type=jnp.float32
        )
        return carry

    lax.fori_loop(0, tiles, states, 0)

    def chain_copy(c):
        return pltpu.make_async_remote_copy(
            src_ref=leaving.at[c],
            dst_ref=arrived.at[c],
            send_sem=chain_send.at[c],
            recv_sem=chain_recv.at[c],
            device_id=(me + 1, z),
            device_id_type=mesh_ids,
        )

    def link(c, carry):
        span = pl.ds(pl.multiple_of(c * tile, tile), tile)

        @pl.when(has_left)
        def _():
            chain_copy(c).wait_recv()

        @pl.when(jnp.logical_not(has_left))
        def _():
            arrived[c] = jnp.zeros_like(arrived[c])

        @pl.when(has_right)
        def _():
            leaving[c] = (
                decay_ref[:, span] * arrived[c].astype(jnp.float32) + local[c]
            ).astype(jnp.bfloat16)
            chain_copy(c).start()

        return carry

    pair = 2 * HEAD_DIM
    causal = lax.broadcasted_iota(jnp.int32, (length, length), 0) >= lax.broadcasted_iota(
        jnp.int32, (length, length), 1
    )

    def within(q, carry):
        span = pl.ds(pl.multiple_of(q * pair, pair), pair)
        value = values[:, span]
        g = lax.div(q * pair, group_width)
        sums = []
        for e in range(2):
            h = 2 * q + e
            lane = lax.broadcasted_iota(jnp.int32, (length, heads), 1)
            column = jnp.sum(jnp.where(lane == h, cum_ref[...], 0.0), axis=1, keepdims=True)
            gap = column - cum_t_ref[pl.ds(h, 1), :]
            kernel = jnp.where(causal, jnp.exp(jnp.where(causal, gap, 0.0)), 0.0)
            mixing = kernel * scores[g] * step_t_ref[pl.ds(h, 1), :]
            sums.append(
                jnp.dot(mixing.astype(jnp.bfloat16), value, preferred_element_type=jnp.float32)
            )
        first = lax.broadcasted_iota(jnp.int32, (length, pair), 1) < HEAD_DIM
        y[:, span] = jnp.where(first, sums[0], sums[1])
        return carry

    late = me >= n // 2

    def phase(turn, carry):
        @pl.when((turn == 0) == late)
        def _():
            lax.fori_loop(0, channels // pair, within, 0)

        @pl.when(turn == 0)
        def _():
            lax.fori_loop(0, tiles, link, 0)

        return carry

    lax.fori_loop(0, 2, phase, 0)

    for g in range(groups_here):
        per = group_width // tile

        def gated(c, squares):
            c = c + g * per
            start = pl.multiple_of(c * tile, tile)
            span = pl.ds(start, tile)
            carried = jnp.dot(
                c_maps[g], arrived[c], preferred_element_type=jnp.float32
            ) * spread(grown, start)
            total = y[:, span] + carried + skip_ref[:, span] * values[:, span].astype(jnp.float32)
            total = total * jax.nn.silu(gate_ref[:, span].astype(jnp.float32))
            y[:, span] = total
            return squares + jnp.sum(total * total, axis=1, keepdims=True)

        squares = lax.fori_loop(0, per, gated, jnp.zeros((length, 1), jnp.float32))
        scale = lax.rsqrt(squares / group_width + 1e-05)

        def scaled(c, carry):
            span = pl.ds(pl.multiple_of((c + g * per) * tile, tile), tile)
            if whole_groups:
                out_ref[:, span] = (y[:, span] * scale * gain_ref[:, span]).astype(out_ref.dtype)
            else:
                out_ref[:, span] = y[:, span]
            return carry

        lax.fori_loop(0, per, scaled, 0)

    @pl.when(has_right)
    def _():
        for which in range(2):
            rim_copy(which).wait_send()

        def sent(c, carry):
            chain_copy(c).wait_send()
            return carry

        lax.fori_loop(0, tiles, sent, 0)


def front(x, gate, maps, cum, step, skip, taps, base, map_taps, map_base, gain, whole_groups):
    n = lax.axis_size("seq")
    length, channels = x.shape
    heads = cum.shape[1]
    per_group = HEADS // GROUPS
    groups_here = max(1, heads // per_group)
    tile = max(128, channels // 8)
    tiles = channels // tile
    rim = 16
    bf16, f32 = jnp.bfloat16, jnp.float32
    dma = pltpu.SemaphoreType.DMA
    vmem = pl.BlockSpec(memory_space=pltpu.VMEM)
    decay = jnp.repeat(jnp.exp(cum[-1]), HEAD_DIM)[None]
    skips = jnp.repeat(skip, HEAD_DIM)[None]
    operands = (
        x, gate, maps, cum, cum.T, step, step.T, decay, skips,
        taps, base[None], map_taps, map_base[None], gain[None],
    )
    return pl.pallas_call(
        functools.partial(front_kernel, n, per_group, whole_groups),
        out_shape=jax.ShapeDtypeStruct((length, channels), bf16 if whole_groups else f32),
        in_specs=[vmem] * len(operands),
        out_specs=vmem,
        scratch_shapes=[
            pltpu.VMEM((rim, channels), bf16),
            pltpu.VMEM((rim, maps.shape[1]), bf16),
            pltpu.VMEM((rim + length, max(tile, STATE)), f32),
            pltpu.VMEM((length, channels), bf16),
            pltpu.VMEM((length, channels), f32),
            pltpu.VMEM((groups_here, length, STATE), bf16),
            pltpu.VMEM((groups_here, length, STATE), bf16),
            pltpu.VMEM((groups_here, length, length), f32),
            pltpu.VMEM((tiles, STATE, tile), f32),
            pltpu.VMEM((tiles, STATE, tile), bf16),
            pltpu.VMEM((tiles, STATE, tile), bf16),
            dma((2,)),
            dma((2,)),
            dma((tiles,)),
            dma((tiles,)),
        ],
        compiler_params=pltpu.CompilerParams(
            collective_id=1, has_side_effects=True, vmem_limit_bytes=48 << 20
        ),
    )(*operands)


def shards(
    conv_values,
    gate_values,
    conv_maps,
    step_raw,
    decay_log,
    skip_gain,
    values_kernel,
    values_offset,
    maps_kernel,
    maps_offset,
    norm_weight,
    out_weight,
    residual,
):
    length = conv_values.shape[0]
    heads_dev = decay_log.shape[0]
    per_group = HEADS // GROUPS
    whole_groups = heads_dev % per_group == 0
    step_size = jax.nn.softplus(step_raw)
    cum_log = jnp.cumsum(-jnp.exp(decay_log)[None, :] * step_size, axis=0)
    normed = front(
        conv_values, gate_values, conv_maps, cum_log, step_size, skip_gain, values_kernel,
        values_offset, maps_kernel, maps_offset, norm_weight, whole_groups,
    )
    if not whole_groups:
        gated_out = normed.reshape(length, heads_dev, HEAD_DIM)
        head_squares = jnp.sum(gated_out * gated_out, axis=2)
        all_heads = lax.all_gather(head_squares, "tp", axis=1, tiled=True)
        group_totals = jnp.sum(all_heads.reshape(length, GROUPS, per_group), axis=2)
        heads_here = lax.axis_index("tp") * heads_dev + jnp.arange(heads_dev, dtype=jnp.int32)
        inv_rms = lax.rsqrt(
            group_totals[:, heads_here // per_group] / (per_group * HEAD_DIM) + 1e-05
        )
        normed = (
            (gated_out * inv_rms[:, :, None]).reshape(length, heads_dev * HEAD_DIM)
            * norm_weight[None, :]
        ).astype(jnp.bfloat16)
    blocks = mix(normed, out_weight)
    summed = jnp.transpose(blocks, (1, 0, 2)).reshape(residual.shape).astype(jnp.float32)
    return residual.astype(jnp.float32) + summed


def solution(mesh):
    placed = (
        P("seq", "tp"),
        P("seq", "tp"),
        P("seq", None),
        P("seq", "tp"),
        P("tp"),
        P("tp"),
        P(None, "tp"),
        P("tp"),
        P(),
        P(),
        P("tp"),
        P("tp", "seq"),
        P(("seq", "tp"), None),
    )
    return jax.shard_map(
        shards, mesh=mesh, in_specs=placed, out_specs=P(("seq", "tp"), None), check_vma=False
    )
```

```python
import functools

import jax
import jax.numpy as jnp
from jax import lax
from jax.experimental import pallas as pl
from jax.experimental.pallas import tpu as pltpu
from jax.sharding import PartitionSpec as P

HEADS = 128
HEAD_DIM = 64
STATE = 128
GROUPS = 8
CONV = 4


def ring_place(spot, size):
    if size % 4:
        return spot
    half = size // 2
    past = spot - half
    turned = half + (half - 2 - 2 * lax.div(past, 2)) + lax.rem(past, 2)
    return jnp.where(spot < half, spot, turned)


def mix_kernel(
    n, m, x_ref, w_ref, out_ref, gat, part, up, down,
    own_sem, gat_send, gat_recv, up_send, up_recv, down_send, down_recv, out_send, out_recv,
):
    mesh_ids = pl.DeviceIdType.MESH
    me, z = lax.axis_index("seq"), lax.axis_index("tp")
    spot = ring_place(me, n)
    right = ring_place(lax.rem(spot + 1, n), n)
    left = ring_place(lax.rem(spot + n - 1, n), n)
    half = gat.shape[2]
    depth = gat.shape[3]
    width = w_ref.shape[1]
    rows = part.shape[1] // m
    tile = min(width, 256)

    own = [
        pltpu.make_async_copy(x_ref.at[pl.ds(d * half, half)], gat.at[0, d], own_sem.at[d])
        for d in range(2)
    ]
    for copy in own:
        copy.start()

    barrier = pltpu.get_barrier_semaphore()

    def greet(step, carry):
        pl.semaphore_signal(
            barrier, inc=1, device_id=(lax.rem(me + step, n), z), device_id_type=mesh_ids
        )
        return carry

    lax.fori_loop(1, n, greet, 0)

    @pl.when(z > 0)
    def _():
        pl.semaphore_signal(barrier, inc=1, device_id=(me, z - 1), device_id_type=mesh_ids)

    @pl.when(z < m - 1)
    def _():
        pl.semaphore_signal(barrier, inc=1, device_id=(me, z + 1), device_id_type=mesh_ids)

    beside = (z > 0).astype(jnp.int32) + (z < m - 1).astype(jnp.int32)
    pl.semaphore_wait(barrier, n - 1 + beside)

    for copy in own:
        copy.wait()

    def gather_copy(step, d):
        return pltpu.make_async_remote_copy(
            src_ref=gat.at[step, d],
            dst_ref=gat.at[step + 1, d],
            send_sem=gat_send.at[step, d],
            recv_sem=gat_recv.at[step + 1, d],
            device_id=(right if d == 0 else left, z),
            device_id_type=mesh_ids,
        )

    def gather_arrival(step, d):
        return pltpu.make_async_remote_copy(
            src_ref=gat.at[step, d],
            dst_ref=gat.at[step, d],
            send_sem=gat_send.at[step, d],
            recv_sem=gat_recv.at[step, d],
            device_id=(right if d == 0 else left, z),
            device_id_type=mesh_ids,
        )

    def chain_copy(step, j, buffer, send, recv, to):
        return pltpu.make_async_remote_copy(
            src_ref=part.at[step, pl.ds(j * rows, rows)],
            dst_ref=buffer.at[step, pl.ds(j * rows, rows)],
            send_sem=send.at[step, j],
            recv_sem=recv.at[step, j],
            device_id=(me, to),
            device_id_type=mesh_ids,
        )

    def owner(step):
        there = jnp.where(z < m // 2, spot - step + n, spot + step)
        return ring_place(lax.rem(there, n), n)

    def out_copy(step, sender):
        return pltpu.make_async_remote_copy(
            src_ref=part.at[step, pl.ds(pl.multiple_of(z * rows, rows), rows)],
            dst_ref=out_ref.at[sender],
            send_sem=out_send.at[step],
            recv_sem=out_recv.at[sender],
            device_id=(owner(step), z),
            device_id_type=mesh_ids,
        )

    def added(step, j, buffer):
        span = pl.ds(j * rows, rows)
        part[step, span] = (
            part[step, span].astype(jnp.float32) + buffer[step, span].astype(jnp.float32)
        ).astype(jnp.bfloat16)

    up_lag, down_lag = z, m - 1 - z
    last_lag = jnp.maximum(up_lag, down_lag)

    def turn(tau, carry):
        @pl.when(tau < n)
        def _():
            @pl.when(tau > 0)
            def _():
                for d in range(2):
                    gather_arrival(tau, d).wait_recv()

            @pl.when(tau < n - 1)
            def _():
                for d in range(2):
                    gather_copy(tau, d).start()

            block = gat[tau].reshape(2 * half, depth)
            for c in range(0, width, tile):
                part[tau, :, c : c + tile] = jnp.dot(
                    block, w_ref[:, c : c + tile], preferred_element_type=jnp.float32
                ).astype(jnp.bfloat16)

        t_up = tau - up_lag

        @pl.when((t_up >= 0) & (t_up < n))
        def _():
            for j in range(m - 1, 0, -1):
                @pl.when(z < j)
                def _():
                    copy = chain_copy(t_up, j, up, up_send, up_recv, z + 1)

                    @pl.when(z > 0)
                    def _():
                        copy.wait_recv()
                        added(t_up, j, up)

                    copy.start()

        t_down = tau - down_lag

        @pl.when((t_down >= 0) & (t_down < n))
        def _():
            for j in range(m - 1):
                @pl.when(z > j)
                def _():
                    copy = chain_copy(t_down, j, down, down_send, down_recv, z - 1)

                    @pl.when(z < m - 1)
                    def _():
                        copy.wait_recv()
                        added(t_down, j, down)

                    copy.start()

        t_last = tau - last_lag

        @pl.when((t_last >= 0) & (t_last < n))
        def _():
            for j in range(m):
                @pl.when(z == j)
                def _():
                    span = pl.ds(j * rows, rows)
                    total = part[t_last, span].astype(jnp.float32)
                    if j > 0:
                        chain_copy(t_last, j, up, up_send, up_recv, z).wait_recv()
                        total = total + up[t_last, span].astype(jnp.float32)
                    if j < m - 1:
                        chain_copy(t_last, j, down, down_send, down_recv, z).wait_recv()
                        total = total + down[t_last, span].astype(jnp.float32)
                    part[t_last, span] = total.astype(jnp.bfloat16)

            @pl.when(t_last == 0)
            def _():
                out_ref[me] = part[0, pl.ds(pl.multiple_of(z * rows, rows), rows)]

            @pl.when(t_last > 0)
            def _():
                out_copy(t_last, me).start()

        return carry

    lax.fori_loop(0, n + m - 1, turn, 0)

    def finish(step, carry):
        @pl.when(step < n - 1)
        def _():
            for d in range(2):
                gather_copy(step, d).wait_send()

        for j in range(m):
            @pl.when(z < j)
            def _():
                chain_copy(step, j, up, up_send, up_recv, z).wait_send()

            @pl.when(z > j)
            def _():
                chain_copy(step, j, down, down_send, down_recv, z).wait_send()

        @pl.when(step > 0)
        def _():
            out_copy(step, me).wait_send()
            out_copy(step, lax.rem(me + step, n)).wait_recv()

        return carry

    lax.fori_loop(0, n, finish, 0)


def mix(normed, weight):
    n, m = lax.axis_size("seq"), lax.axis_size("tp")
    length, depth = normed.shape
    width = weight.shape[1]
    rows = length // m
    half = length // 2
    slots = pltpu.VMEM((n, length, width), jnp.bfloat16)
    dma = pltpu.SemaphoreType.DMA
    vmem = pl.BlockSpec(memory_space=pltpu.VMEM)
    return pl.pallas_call(
        functools.partial(mix_kernel, n, m),
        out_shape=jax.ShapeDtypeStruct((n, rows, width), jnp.bfloat16),
        in_specs=[pl.BlockSpec(memory_space=pl.ANY), vmem],
        out_specs=vmem,
        scratch_shapes=[
            pltpu.VMEM((n, 2, half, depth), jnp.bfloat16),
            slots,
            slots,
            slots,
            dma((2,)),
            dma((n, 2)),
            dma((n, 2)),
            dma((n, m)),
            dma((n, m)),
            dma((n, m)),
            dma((n, m)),
            dma((n,)),
            dma((n,)),
        ],
        compiler_params=pltpu.CompilerParams(
            collective_id=0, has_side_effects=True, vmem_limit_bytes=48 << 20
        ),
        cost_estimate=pl.CostEstimate(
            flops=2 * n * length * depth * width,
            bytes_accessed=2 * (depth * width + length * depth),
            transcendentals=0,
        ),
    )(normed, weight)


def front_kernel(
    n, per_group, whole_groups, x_hbm, gate_hbm, maps_hbm, taps_hbm, base_hbm, map_taps_hbm,
    map_base_hbm, gain_hbm, cum_ref, cum_t_ref, step_ref, step_t_ref, decay_ref, skip_ref, out_ref,
    x_ref, gate_ref, maps_ref, taps_ref, base_ref, map_taps_ref, map_base_ref, gain_ref,
    load_sem, rim_x, rim_maps, pad, values, y, b_maps, c_maps, scores, local, arrived, leaving,
    rim_send, rim_recv, chain_send, chain_recv,
):
    mesh_ids = pl.DeviceIdType.MESH
    exact = lax.Precision.HIGHEST
    me, z = lax.axis_index("seq"), lax.axis_index("tp")
    length, channels = x_ref.shape
    heads = cum_ref.shape[1]
    groups_here = scores.shape[0]
    first_group = lax.div(z * heads, per_group)
    tile = arrived.shape[2]
    tiles = channels // tile
    group_width = channels // groups_here
    rim = rim_x.shape[0]

    loads = [
        pltpu.make_async_copy(source, target, load_sem.at[i])
        for i, (source, target) in enumerate(
            (
                (maps_hbm, maps_ref),
                (map_taps_hbm, map_taps_ref),
                (map_base_hbm, map_base_ref),
                (x_hbm, x_ref),
                (taps_hbm, taps_ref),
                (base_hbm, base_ref),
                (gate_hbm, gate_ref),
                (gain_hbm, gain_ref),
            )
        )
    ]
    for load in loads:
        load.start()

    barrier = pltpu.get_barrier_semaphore()
    has_left, has_right = me > 0, me < n - 1

    @pl.when(has_left)
    def _():
        pl.semaphore_signal(barrier, inc=1, device_id=(me - 1, z), device_id_type=mesh_ids)

    @pl.when(has_right)
    def _():
        pl.semaphore_signal(barrier, inc=1, device_id=(me + 1, z), device_id_type=mesh_ids)

    pl.semaphore_wait(barrier, has_left.astype(jnp.int32) + has_right.astype(jnp.int32))

    def rim_copy(which):
        source, target = ((x_hbm, rim_x), (maps_hbm, rim_maps))[which]
        return pltpu.make_async_remote_copy(
            src_ref=source.at[pl.ds(length - rim, rim)],
            dst_ref=target,
            send_sem=rim_send.at[which],
            recv_sem=rim_recv.at[which],
            device_id=(me + 1, z),
            device_id_type=mesh_ids,
        )

    @pl.when(has_right)
    def _():
        for which in range(2):
            rim_copy(which).start()

    for load in loads:
        load.wait()

    @pl.when(has_left)
    def _():
        for which in range(2):
            rim_copy(which).wait_recv()

    @pl.when(jnp.logical_not(has_left))
    def _():
        rim_x[...] = jnp.zeros_like(rim_x)
        rim_maps[...] = jnp.zeros_like(rim_maps)

    def conv(rows_ref, rim_ref, taps, base, start, size):
        span = pl.ds(start, size)
        pad[0:rim, 0:size] = rim_ref[:, span].astype(jnp.float32)
        pad[rim : rim + length, 0:size] = rows_ref[:, span].astype(jnp.float32)
        total = base[:, span]
        for k in range(CONV):
            at = rim - (CONV - 1) + k
            total = total + taps[k : k + 1, span] * pad[at : at + length, 0:size]
        return jax.nn.silu(total).astype(jnp.bfloat16)

    for g in range(groups_here):
        at = pl.multiple_of((first_group + g) * STATE, STATE)
        b_maps[g] = conv(maps_ref, rim_maps, map_taps_ref, map_base_ref, at, STATE)
        at = pl.multiple_of((GROUPS + first_group + g) * STATE, STATE)
        c_maps[g] = conv(maps_ref, rim_maps, map_taps_ref, map_base_ref, at, STATE)
        scores[g] = lax.dot_general(
            c_maps[g], b_maps[g], (((1,), (1,)), ((), ())), preferred_element_type=jnp.float32
        )

    def spread(per_head, start):
        head = lax.broadcasted_iota(jnp.int32, (heads, tile), 0) * HEAD_DIM
        lane = lax.broadcasted_iota(jnp.int32, (heads, tile), 1) + start
        chosen = ((lane >= head) & (lane < head + HEAD_DIM)).astype(jnp.float32)
        return jnp.dot(
            per_head, chosen, precision=exact, preferred_element_type=jnp.float32
        )

    cum = cum_ref[...]
    end_weight = jnp.exp(cum[length - 1 : length] - cum) * step_ref[...]
    grown = jnp.exp(cum)

    late = me >= n // 2

    def chain_copy(c):
        return pltpu.make_async_remote_copy(
            src_ref=leaving.at[c],
            dst_ref=arrived.at[c],
            send_sem=chain_send.at[c],
            recv_sem=chain_recv.at[c],
            device_id=(me + 1, z),
            device_id_type=mesh_ids,
        )

    def link(c, carry):
        span = pl.ds(pl.multiple_of(c * tile, tile), tile)

        @pl.when(has_left)
        def _():
            chain_copy(c).wait_recv()

        @pl.when(jnp.logical_not(has_left))
        def _():
            arrived[c] = jnp.zeros_like(arrived[c])

        @pl.when(has_right)
        def _():
            leaving[c] = (
                decay_ref[:, span] * arrived[c].astype(jnp.float32) + local[c]
            ).astype(jnp.bfloat16)
            chain_copy(c).start()

        return carry

    def states(c, carry):
        start = pl.multiple_of(c * tile, tile)
        span = pl.ds(start, tile)
        value = conv(x_ref, rim_x, taps_ref, base_ref, start, tile)
        values[:, span] = value
        weighted = (value.astype(jnp.float32) * spread(end_weight, start)).astype(jnp.bfloat16)
        g = lax.div(start, group_width)
        local[c] = lax.dot_general(
            b_maps[g], weighted, (((0,), (0,)), ((), ())), preferred_element_type=jnp.float32
        )

        @pl.when(jnp.logical_not(late))
        def _():
            link(c, 0)

        return carry

    lax.fori_loop(0, tiles, states, 0)

    pair = 2 * HEAD_DIM
    causal = lax.broadcasted_iota(jnp.int32, (length, length), 0) >= lax.broadcasted_iota(
        jnp.int32, (length, length), 1
    )

    def within(q, carry):
        span = pl.ds(pl.multiple_of(q * pair, pair), pair)
        value = values[:, span]
        g = lax.div(q * pair, group_width)
        sums = []
        for e in range(2):
            h = 2 * q + e
            lane = lax.broadcasted_iota(jnp.int32, (length, heads), 1)
            column = jnp.sum(jnp.where(lane == h, cum_ref[...], 0.0), axis=1, keepdims=True)
            gap = column - cum_t_ref[pl.ds(h, 1), :]
            kernel = jnp.where(causal, jnp.exp(jnp.where(causal, gap, 0.0)), 0.0)
            mixing = kernel * scores[g] * step_t_ref[pl.ds(h, 1), :]
            sums.append(
                jnp.dot(mixing.astype(jnp.bfloat16), value, preferred_element_type=jnp.float32)
            )
        first = lax.broadcasted_iota(jnp.int32, (length, pair), 1) < HEAD_DIM
        y[:, span] = jnp.where(first, sums[0], sums[1])
        return carry

    lax.fori_loop(0, channels // pair, within, 0)

    @pl.when(late)
    def _():
        lax.fori_loop(0, tiles, link, 0)

    for g in range(groups_here):
        per = group_width // tile

        def gated(c, squares):
            c = c + g * per
            start = pl.multiple_of(c * tile, tile)
            span = pl.ds(start, tile)
            carried = jnp.dot(
                c_maps[g], arrived[c], preferred_element_type=jnp.float32
            ) * spread(grown, start)
            total = y[:, span] + carried + skip_ref[:, span] * values[:, span].astype(jnp.float32)
            total = total * jax.nn.silu(gate_ref[:, span].astype(jnp.float32))
            y[:, span] = total
            return squares + jnp.sum(total * total, axis=1, keepdims=True)

        squares = lax.fori_loop(0, per, gated, jnp.zeros((length, 1), jnp.float32))
        scale = lax.rsqrt(squares / group_width + 1e-05)

        def scaled(c, carry):
            span = pl.ds(pl.multiple_of((c + g * per) * tile, tile), tile)
            if whole_groups:
                out_ref[:, span] = (y[:, span] * scale * gain_ref[:, span]).astype(out_ref.dtype)
            else:
                out_ref[:, span] = y[:, span]
            return carry

        lax.fori_loop(0, per, scaled, 0)

    @pl.when(has_right)
    def _():
        for which in range(2):
            rim_copy(which).wait_send()

        def sent(c, carry):
            chain_copy(c).wait_send()
            return carry

        lax.fori_loop(0, tiles, sent, 0)


def front(x, gate, maps, cum, step, skip, taps, base, map_taps, map_base, gain, whole_groups):
    n = lax.axis_size("seq")
    length, channels = x.shape
    heads = cum.shape[1]
    per_group = HEADS // GROUPS
    groups_here = max(1, heads // per_group)
    tile = max(128, channels // 8)
    tiles = channels // tile
    rim = 16
    bf16, f32 = jnp.bfloat16, jnp.float32
    dma = pltpu.SemaphoreType.DMA
    vmem = pl.BlockSpec(memory_space=pltpu.VMEM)
    decay = jnp.repeat(jnp.exp(cum[-1]), HEAD_DIM)[None]
    skips = jnp.repeat(skip, HEAD_DIM)[None]
    operands = (
        x, gate, maps, taps, base[None], map_taps, map_base[None], gain[None],
        cum, cum.T, step, step.T, decay, skips,
    )
    loaded = operands[:8]
    return pl.pallas_call(
        functools.partial(front_kernel, n, per_group, whole_groups),
        out_shape=jax.ShapeDtypeStruct((length, channels), bf16 if whole_groups else f32),
        in_specs=[pl.BlockSpec(memory_space=pltpu.HBM)] * len(loaded)
        + [vmem] * (len(operands) - len(loaded)),
        out_specs=vmem,
        scratch_shapes=[pltpu.VMEM(array.shape, array.dtype) for array in loaded]
        + [
            dma((len(loaded),)),
            pltpu.VMEM((rim, channels), bf16),
            pltpu.VMEM((rim, maps.shape[1]), bf16),
            pltpu.VMEM((rim + length, max(tile, STATE)), f32),
            pltpu.VMEM((length, channels), bf16),
            pltpu.VMEM((length, channels), f32),
            pltpu.VMEM((groups_here, length, STATE), bf16),
            pltpu.VMEM((groups_here, length, STATE), bf16),
            pltpu.VMEM((groups_here, length, length), f32),
            pltpu.VMEM((tiles, STATE, tile), f32),
            pltpu.VMEM((tiles, STATE, tile), bf16),
            pltpu.VMEM((tiles, STATE, tile), bf16),
            dma((2,)),
            dma((2,)),
            dma((tiles,)),
            dma((tiles,)),
        ],
        compiler_params=pltpu.CompilerParams(
            collective_id=1, has_side_effects=True, vmem_limit_bytes=48 << 20
        ),
    )(*operands)


def shards(
    conv_values,
    gate_values,
    conv_maps,
    step_raw,
    decay_log,
    skip_gain,
    values_kernel,
    values_offset,
    maps_kernel,
    maps_offset,
    norm_weight,
    out_weight,
    residual,
):
    length = conv_values.shape[0]
    heads_dev = decay_log.shape[0]
    per_group = HEADS // GROUPS
    whole_groups = heads_dev % per_group == 0
    step_size = jax.nn.softplus(step_raw)
    cum_log = jnp.cumsum(-jnp.exp(decay_log)[None, :] * step_size, axis=0)
    normed = front(
        conv_values, gate_values, conv_maps, cum_log, step_size, skip_gain, values_kernel,
        values_offset, maps_kernel, maps_offset, norm_weight, whole_groups,
    )
    if not whole_groups:
        gated_out = normed.reshape(length, heads_dev, HEAD_DIM)
        head_squares = jnp.sum(gated_out * gated_out, axis=2)
        all_heads = lax.all_gather(head_squares, "tp", axis=1, tiled=True)
        group_totals = jnp.sum(all_heads.reshape(length, GROUPS, per_group), axis=2)
        heads_here = lax.axis_index("tp") * heads_dev + jnp.arange(heads_dev, dtype=jnp.int32)
        inv_rms = lax.rsqrt(
            group_totals[:, heads_here // per_group] / (per_group * HEAD_DIM) + 1e-05
        )
        normed = (
            (gated_out * inv_rms[:, :, None]).reshape(length, heads_dev * HEAD_DIM)
            * norm_weight[None, :]
        ).astype(jnp.bfloat16)
    blocks = mix(normed, out_weight)
    summed = jnp.transpose(blocks, (1, 0, 2)).reshape(residual.shape).astype(jnp.float32)
    return residual.astype(jnp.float32) + summed


def solution(mesh):
    placed = (
        P("seq", "tp"),
        P("seq", "tp"),
        P("seq", None),
        P("seq", "tp"),
        P("tp"),
        P("tp"),
        P(None, "tp"),
        P("tp"),
        P(),
        P(),
        P("tp"),
        P("tp", "seq"),
        P(("seq", "tp"), None),
    )
    return jax.shard_map(
        shards, mesh=mesh, in_specs=placed, out_specs=P(("seq", "tp"), None), check_vma=False
    )
```
